32 devices in a mesh: chan: 8 (over z, core), tile: 4 (over y, x).
Axes of the slice: x: 2, y: 2, z: 4, core: 2. Of those that a mesh axis runs over, the one named last changes fastest.
Arguments:
- voltages: bfloat16 [262144, 2048], P('chan', 'tile'), may hold values from -4 to 4
- pfb_taps: float32 [4, 2048], replicated, may hold values from -3 to 3
Outputs:
- visibility: float32 [16, 2, 2048, 2048], P('chan', None, 'tile')
The draws below stay inside these ranges and needn't reach their ends.
All inputs are finite; a program needn't handle non-finite values.
Results may differ from the reference program's by a relative error of at most 0.0038.
Values may be sent and summed in bfloat16 or wider, within the bound.
No kernel may reach another device: no remote copies, remote signals or barrier semaphores. Data moves between devices by JAX's collectives and lax.ppermute only.
A program may use at most 256 MiB of HBM per device.

```python
import math
import jax
import jax.numpy as jnp
from jax import lax

INPUTS = 2048
FFT_LEN = 2048
TAPS = 4
CHANNELS = 16
SPECTRA = 128
TIME = 262144


def block_levels(stream_key, extent, pieces, least, high):
    def one(axis_at, parts):
        heights = jax.random.uniform(jax.random.fold_in(jax.random.fold_in(stream_key, 6), axis_at), (parts,), jnp.float32, least / len(pieces), high / len(pieces))
        return jnp.repeat(jnp.exp(heights), extent[axis_at] // parts).reshape((-1,) + (1,) * (len(extent) - axis_at - 1))

    gain = one(*pieces[0])
    for cut in pieces[1:]:
        gain = gain * one(*cut)
    return gain


def normal_values(stream_key, dims, spread, most, cuts=(), kind=jnp.bfloat16):
    values = spread * jax.random.normal(stream_key, dims, jnp.float32)
    if cuts:
        values = values * block_levels(stream_key, dims, cuts, -0.22, 0.18)
    return jnp.clip(values, -most, most).astype(kind)


def setup_inputs(seed: int = 0) -> dict:
    key_list = jax.random.split(jax.random.key(seed), 3)
    voltages = normal_values(key_list[0], (TIME, INPUTS), 1.0, 4.0, ((0, 8), (1, 4)))
    pfb_taps = normal_values(key_list[1], (TAPS, FFT_LEN), 0.5, 3.0, (), jnp.float32)
    return {"voltages": voltages, "pfb_taps": pfb_taps}


def dft_table(frame_len, channel_count):
    samples = jnp.arange(frame_len, dtype=jnp.int32)
    centers = frame_len // 8 + jnp.arange(channel_count, dtype=jnp.int32)
    phase_index = samples[:, None] * centers[None, :] % frame_len
    angle = 2.0 * jnp.pi / frame_len * phase_index.astype(jnp.float32)
    factor = 1.0 / math.sqrt(frame_len)
    return jnp.concatenate([jnp.cos(angle) * factor, -jnp.sin(angle) * factor], axis=1)

def reference(voltages, pfb_taps):
    table = dft_table(FFT_LEN, CHANNELS)
    padded = jnp.concatenate([voltages, jnp.zeros(((TAPS - 1) * FFT_LEN, INPUTS), voltages.dtype)], axis=0)

    def one_spectrum(spec_index):
        samples = lax.dynamic_slice_in_dim(padded, spec_index * FFT_LEN, TAPS * FFT_LEN, 0)
        window = samples.astype(jnp.float32).reshape(TAPS, FFT_LEN, INPUTS)
        filtered = lax.optimization_barrier(jnp.sum(pfb_taps[:, :, None] * window, axis=0))
        return jnp.dot(table.T, filtered, precision=lax.Precision.HIGHEST, preferred_element_type=jnp.float32)
    spectra = lax.map(one_spectrum, jnp.arange(SPECTRA, dtype=jnp.int32))
    spectra = spectra.astype(jnp.bfloat16).reshape(SPECTRA, 2, CHANNELS, INPUTS)
    by_channel = jnp.transpose(spectra, (2, 0, 1, 3))

    def one_channel(samples):
        values = samples.astype(jnp.float32)
        products = jnp.einsum('sai,sbk->aibk', values, values, precision=lax.Precision.HIGHEST)
        real_part = products[0, :, 0, :] + products[1, :, 1, :]
        imag_part = products[1, :, 0, :] - products[0, :, 1, :]
        return jnp.stack([real_part, imag_part], axis=0) / SPECTRA
    return lax.map(one_channel, by_channel)
```

```python
import functools
import math

import jax
import jax.numpy as jnp
import numpy as np
from jax import lax
from jax.experimental import pallas as pl
from jax.experimental.pallas import tpu as pltpu
from jax.sharding import PartitionSpec as P

CH_DEV = 2
PARTS = 2 * CH_DEV
SLOTS = 6
UNROLL = 2
VMEM_LIMIT = 60 * 1024 * 1024


def dft_table(frame_len, channel_count):
    samples = np.arange(frame_len)
    centers = frame_len // 8 + np.arange(channel_count)
    angle = 2.0 * np.pi / frame_len * (centers[:, None] * samples[None, :] % frame_len)
    table = np.stack([np.cos(angle), -np.sin(angle)], axis=1) / math.sqrt(frame_len)
    return table.reshape(2 * channel_count, frame_len).astype(np.float32)


def channelize_kernel(taps, frames, me_ref, table_ref, taps_ref, v_ref, *refs):
    outs, (buf, w, acc, rows, sems) = refs[:-5], refs[-5:]
    group, frame_len = table_ref.shape
    width = buf.shape[2]
    over = taps - 1
    half = taps * group
    me = me_ref[0]
    count = len(outs)

    def fetch(f, slot):
        return pltpu.make_async_copy(v_ref.at[pl.ds(f * frame_len, frame_len), :], buf.at[slot], sems.at[slot])

    for f in range(min(SLOTS - 1, frames)):
        fetch(f, f).start()

    for t in range(taps):
        folded = table_ref[...] * taps_ref[t : t + 1, :]
        high = folded.astype(jnp.bfloat16)
        w[t * group : (t + 1) * group, :] = high
        w[half + t * group : half + (t + 1) * group, :] = (folded - high.astype(jnp.float32)).astype(jnp.bfloat16)
    acc[...] = jnp.zeros_like(acc)

    pitch = rows.shape[1] // group

    def put(slot, value, start):
        for lane in range(0, value.shape[1], 128):
            for c in range(0, group, 8):
                rows[(start + lane) // 128, pl.ds(c * pitch + slot, 8, stride=pitch), :] = value[c : c + 8, lane : lane + 128]

    step = min(256, width)

    def frame(f):
        slot = lax.rem(f, SLOTS)

        @pl.when(f + SLOTS - 1 < frames)
        def _():
            fetch(f + SLOTS - 1, lax.rem(f + SLOTS - 1, SLOTS)).start()

        fetch(f, slot).wait()
        to = jnp.where(f < over, frames + f, f - over)
        for start in range(0, width, step):
            cols = pl.ds(start, step)
            both = jnp.dot(w[...], buf[slot, :, cols], preferred_element_type=jnp.float32)
            y = both[:half] + both[half:]
            part = [y[t * group : (t + 1) * group] for t in range(taps)]
            put(to, acc[0, :, cols] + part[over], start)
            for t in range(over - 1):
                acc[t, :, cols] = acc[t + 1, :, cols] + part[over - 1 - t]
            acc[over - 1, :, cols] = part[0]

    def some(g, carry):
        for k in range(UNROLL):
            frame(g * UNROLL + k)
        return carry

    lax.fori_loop(0, frames // UNROLL, some, 0)
    for t in range(over):
        put(frames - over + t, acc[t], 0)
    keep = jnp.where(me == 0, 0.0, 1.0)
    for d, out in enumerate(outs):
        dest = lax.rem(me - d + count, count)
        for lane in range(0, width, 128):
            share = []
            for q in range(PARTS):
                at = pl.multiple_of(dest * (PARTS * pitch), 8) + q * pitch
                got = rows[lane // 128, pl.ds(at, pitch), :]
                out[q * frames : (q + 1) * frames, lane : lane + 128] = got[:frames].astype(out.dtype)
                share.append(got[frames : frames + taps] * keep)
            out[PARTS * frames :, lane : lane + 128] = jnp.concatenate(share, axis=0).astype(out.dtype)


def channelize(voltages, pfb_taps, chan_count):
    taps, frame_len = pfb_taps.shape
    frames = voltages.shape[0] // frame_len
    width = voltages.shape[1]
    group = chan_count * PARTS
    piece = (PARTS * (frames + taps), width)
    me = lax.axis_index("chan").astype(jnp.int32).reshape(1)
    vmem = pl.BlockSpec(memory_space=pltpu.VMEM)
    return pl.pallas_call(
        functools.partial(channelize_kernel, taps, frames),
        in_specs=[pl.BlockSpec(memory_space=pltpu.SMEM), vmem, vmem, pl.BlockSpec(memory_space=pl.ANY)],
        out_specs=[vmem] * chan_count,
        out_shape=[jax.ShapeDtypeStruct(piece, jnp.bfloat16)] * chan_count,
        scratch_shapes=[
            pltpu.VMEM((SLOTS, frame_len, width), jnp.bfloat16),
            pltpu.VMEM((2 * taps * group, frame_len), jnp.bfloat16),
            pltpu.VMEM((taps - 1, group, width), jnp.float32),
            pltpu.VMEM((width // 128, group * (frames + 8), 128), jnp.float32),
            pltpu.SemaphoreType.DMA((SLOTS,)),
        ],
        compiler_params=pltpu.CompilerParams(vmem_limit_bytes=VMEM_LIMIT),
        cost_estimate=pl.CostEstimate(
            flops=4 * taps * group * frame_len * frames * width,
            bytes_accessed=2 * voltages.size,
            transcendentals=0,
        ),
        name="channelize",
    )(me, dft_table(frame_len, CH_DEV * chan_count), pfb_taps, voltages)


def pack_kernel(taps, frames, *refs):
    pieces, out = refs[:-1], refs[-1]
    over = taps - 1
    width = out.shape[3]
    late = lax.broadcasted_iota(jnp.int32, (frames, width), 0) >= frames - over
    extra = PARTS * taps
    for d in range(len(pieces) - 1):
        shares = pieces[d + 1][PARTS * frames :, :].astype(jnp.float32)
        for q in range(PARTS):
            body = pieces[d][q * frames : (q + 1) * frames, :].astype(jnp.float32)
            moved = pltpu.roll(shares, (frames - over - q * taps) % extra, 0)
            out[q // 2, q % 2, d * frames : (d + 1) * frames, :] = (body + jnp.where(late, moved, 0.0)).astype(out.dtype)


def pack(pieces, taps, frames):
    width = pieces[0].shape[1]
    count = len(pieces) - 1
    return pl.pallas_call(
        functools.partial(pack_kernel, taps, frames),
        in_specs=[pl.BlockSpec(memory_space=pltpu.VMEM)] * len(pieces),
        out_shape=jax.ShapeDtypeStruct((CH_DEV, 2, count * frames, width), jnp.bfloat16),
        compiler_params=pltpu.CompilerParams(vmem_limit_bytes=8 << 20),
        cost_estimate=pl.CostEstimate(flops=0, bytes_accessed=4 * count * pieces[0].size, transcendentals=0),
        name="pack",
    )(*pieces)


def fill_left(scale, left, halves):
    for c in range(CH_DEV):
        both = jnp.concatenate([x[c, k] for k in range(2) for x in halves], axis=0).T * scale
        rows, depth = both.shape[0], both.shape[1] // 2
        left[c, :rows, :] = both
        left[c, rows:, :depth] = both[:, depth:]
        left[c, rows:, depth:] = -both[:, :depth]


def correlate_kernel(scales, count, step, index_ref, *refs):
    held, sems = refs[-2:]
    first = len(refs) == 2 * count + 4
    if first:
        blocks, (out, left) = refs[: 2 * count], refs[-4:-2]
        fill_left(scales[0], left, blocks)
    else:
        left, blocks, out = refs[0], refs[1 : 1 + 2 * count], refs[-3]
    rows, width = held.shape[2], held.shape[3]
    parts = width // step
    sent = []
    for k in range(count):
        base = index_ref[k] * width
        for c in range(CH_DEV):
            for n in range(parts):
                cols = slice(n * step, (n + 1) * step)
                right = jnp.concatenate([x[c, p, :, cols] for p in range(2) for x in blocks[2 * k : 2 * k + 2]], axis=0)
                for p in range(2):
                    slot = (k * CH_DEV + c) * 2 + p
                    res = jnp.dot(left[c, p * rows : (p + 1) * rows], right, preferred_element_type=jnp.float32)
                    held[slot // 2, p, :, cols] = res if scales[1] == 1.0 else res * scales[1]
                    copy = pltpu.make_async_copy(
                        held.at[slot // 2, p, :, cols],
                        out.at[c, p, :, pl.ds(pl.multiple_of(base + n * step, step), step)],
                        sems.at[slot * parts + n],
                    )
                    copy.start()
                    sent.append(copy)
    for copy in sent:
        copy.wait()


def correlate(left, blocks, index, so_far, tiles, total):
    chans, _, _, width = blocks[0][0].shape
    count = len(blocks)
    flat = [x for pair in blocks for x in pair]
    full = 2 * sum(x.shape[2] for x in blocks[0])
    step = min(256, width)
    exact = total & (total - 1) == 0
    scales = (1.0 / total, 1.0) if exact else (1.0, 1.0 / total)
    vmem = pl.BlockSpec(memory_space=pltpu.VMEM)
    anywhere = pl.BlockSpec(memory_space=pl.ANY)
    shape = jax.ShapeDtypeStruct((chans, 2, width, tiles * width), jnp.float32)
    first = left is None
    slots = chans * count
    ins = [vmem] * len(flat) if first else [vmem] * (1 + len(flat)) + [anywhere]
    return pl.pallas_call(
        functools.partial(correlate_kernel, scales, count, step),
        in_specs=[pl.BlockSpec(memory_space=pltpu.SMEM)] + ins,
        out_specs=[anywhere, vmem] if first else anywhere,
        out_shape=[shape, jax.ShapeDtypeStruct((chans, 2 * width, full), jnp.bfloat16)] if first else shape,
        scratch_shapes=[
            pltpu.VMEM((slots, 2, width, width), jnp.float32),
            pltpu.SemaphoreType.DMA((2 * slots * (width // step),)),
        ],
        input_output_aliases={} if first else {2 + len(flat): 0},
        compiler_params=pltpu.CompilerParams(vmem_limit_bytes=(2 * slots * width * width * 4) + (8 << 20)),
        cost_estimate=pl.CostEstimate(
            flops=4 * count * chans * width * width * full,
            bytes_accessed=8 * count * chans * width * width,
            transcendentals=0,
        ),
        name="correlate",
    )(*((index, *flat) if first else (index, left, *flat, so_far)))


def shift(block, axis, distance):
    count = lax.axis_size(axis)
    return lax.ppermute(block, axis, [(i, (i - distance) % count) for i in range(count)])


def gather(block, axis, bits):
    count = lax.axis_size(axis)
    got = {0: block}
    for bit in bits:
        for e in list(got):
            got[e | bit] = lax.ppermute(got[e], axis, [(i, i ^ bit) for i in range(count)])
    return got


def shards(voltages, pfb_taps):
    chan_count = lax.axis_size("chan")
    tiles = lax.axis_size("tile")
    taps, frame_len = pfb_taps.shape
    frames = voltages.shape[0] // frame_len
    sent = channelize(voltages, pfb_taps, chan_count)
    got = [sent[0]] + [shift(sent[d], "chan", d) for d in range(1, chan_count)]
    cut = chan_count // 2
    early = pack(got[: cut + 1], taps, frames)
    late = pack(got[cut:] + got[:1], taps, frames)
    bits = [1 << k for k in range(tiles.bit_length() - 1)]
    one = gather(early, "tile", bits)
    two = gather(late, "tile", bits[::-1])
    me = lax.axis_index("tile").astype(jnp.int32)
    total = chan_count * frames
    out, left = correlate(None, [(early, late)], me.reshape(1), None, tiles, total)
    for group in (bits, [e for e in range(1, tiles) if e not in bits]):
        index = me ^ jnp.array(group, jnp.int32)
        out = correlate(left, [(one[e], two[e]) for e in group], index, out, tiles, total)
    return out


def solution(mesh):
    placed = (P("chan", "tile"), P())
    return jax.shard_map(
        shards, mesh=mesh, in_specs=placed, out_specs=P("chan", None, "tile", None), check_vma=False
    )
```

```python
import functools
import math

import jax
import jax.numpy as jnp
import numpy as np
from jax import lax
from jax.experimental import pallas as pl
from jax.experimental.pallas import tpu as pltpu
from jax.sharding import PartitionSpec as P

CH_DEV = 2
PARTS = 2 * CH_DEV
SLOTS = 6
UNROLL = 2
LOW_TAPS = 4


def dft_table(frame_len, channel_count):
    samples = np.arange(frame_len)
    centers = frame_len // 8 + np.arange(channel_count)
    angle = 2.0 * np.pi / frame_len * (centers[:, None] * samples[None, :] % frame_len)
    table = np.stack([np.cos(angle), -np.sin(angle)], axis=1) / math.sqrt(frame_len)
    return table.reshape(2 * channel_count, frame_len).astype(np.float32)


def channelize_kernel(taps, frames, me_ref, table_hbm, taps_hbm, v_ref, *refs):
    outs, (buf, w, acc, rows, table_ref, taps_ref, sems, early) = refs[:-8], refs[-8:]
    group, frame_len = table_ref.shape
    width = buf.shape[2]
    over = taps - 1
    half = taps * group
    me = me_ref[0]

    def fetch(f, slot):
        return pltpu.make_async_copy(v_ref.at[pl.ds(f * frame_len, frame_len), :], buf.at[slot], sems.at[slot])

    small = [
        pltpu.make_async_copy(table_hbm, table_ref, early.at[0]),
        pltpu.make_async_copy(taps_hbm, taps_ref, early.at[1]),
    ]
    for copy in small:
        copy.start()
    for f in range(min(SLOTS - 1, frames)):
        fetch(f, f).start()
    acc[...] = jnp.zeros_like(acc)
    for copy in small:
        copy.wait()

    for t in range(taps):
        folded = table_ref[...] * taps_ref[t : t + 1, :]
        high = folded.astype(jnp.bfloat16)
        w[t * group : (t + 1) * group, :] = high
        if t < LOW_TAPS:
            low = folded - high.astype(jnp.float32)
            w[half + t * group : half + (t + 1) * group, :] = low.astype(jnp.bfloat16)

    pitch = rows.shape[1] // group

    def put(slot, value, start):
        for lane in range(0, value.shape[1], 128):
            for c in range(0, group, 8):
                rows[(start + lane) // 128, pl.ds(c * pitch + slot, 8, stride=pitch), :] = value[c : c + 8, lane : lane + 128]

    step = min(256, width)

    def frame(f):
        slot = lax.rem(f, SLOTS)

        @pl.when(f + SLOTS - 1 < frames)
        def _():
            fetch(f + SLOTS - 1, lax.rem(f + SLOTS - 1, SLOTS)).start()

        fetch(f, slot).wait()
        to = jnp.where(f < over, frames + f, f - over)
        for start in range(0, width, step):
            cols = pl.ds(start, step)
            both = jnp.dot(w[...], buf[slot, :, cols], preferred_element_type=jnp.float32)
            part = [both[t * group : (t + 1) * group] for t in range(taps)]
            for t in range(LOW_TAPS):
                part[t] = part[t] + both[half + t * group : half + (t + 1) * group]
            put(to, acc[0, :, cols] + part[over], start)
            for t in range(over - 1):
                acc[t, :, cols] = acc[t + 1, :, cols] + part[over - 1 - t]
            acc[over - 1, :, cols] = part[0]

    def some(g, carry):
        for k in range(UNROLL):
            frame(g * UNROLL + k)
        return carry

    lax.fori_loop(0, frames // UNROLL, some, 0)
    for t in range(over):
        put(frames - over + t, acc[t], 0)
    keep = jnp.where(me == 0, 0.0, 1.0)
    pairs = group // PARTS // 2
    size = PARTS * (frames + taps)
    core = lax.rem(me, 2)
    for flip, out in enumerate(outs):
        for e in range(pairs):
            dest = 2 * lax.rem(lax.div(me, 2) - e + pairs, pairs) + (1 - core if flip else core)
            for lane in range(0, width, 128):
                share = []
                for q in range(PARTS):
                    at = pl.multiple_of(dest * (PARTS * pitch), 8) + q * pitch
                    got = rows[lane // 128, pl.ds(at, pitch), :]
                    to = e * size + q * frames
                    out[to : to + frames, lane : lane + 128] = got[:frames].astype(out.dtype)
                    share.append(got[frames : frames + taps] * keep)
                to = e * size + PARTS * frames
                out[to : to + PARTS * taps, lane : lane + 128] = jnp.concatenate(share, axis=0).astype(out.dtype)


def channelize(voltages, pfb_taps, chan_count):
    taps, frame_len = pfb_taps.shape
    frames = voltages.shape[0] // frame_len
    width = voltages.shape[1]
    group = chan_count * PARTS
    piece = (chan_count // 2 * PARTS * (frames + taps), width)
    table = jnp.asarray(dft_table(frame_len, CH_DEV * chan_count))
    me = lax.axis_index("chan").astype(jnp.int32).reshape(1)
    vmem = pl.BlockSpec(memory_space=pltpu.VMEM)
    return pl.pallas_call(
        functools.partial(channelize_kernel, taps, frames),
        in_specs=[pl.BlockSpec(memory_space=pltpu.SMEM)] + [pl.BlockSpec(memory_space=pltpu.HBM)] * 3,
        out_specs=[vmem] * 2,
        out_shape=[jax.ShapeDtypeStruct(piece, jnp.bfloat16)] * 2,
        scratch_shapes=[
            pltpu.VMEM((SLOTS, frame_len, width), jnp.bfloat16),
            pltpu.VMEM(((taps + LOW_TAPS) * group, frame_len), jnp.bfloat16),
            pltpu.VMEM((taps - 1, group, width), jnp.float32),
            pltpu.VMEM((width // 128, group * (frames + 8), 128), jnp.float32),
            pltpu.VMEM((group, frame_len), jnp.float32),
            pltpu.VMEM((taps, frame_len), jnp.float32),
            pltpu.SemaphoreType.DMA((SLOTS,)),
            pltpu.SemaphoreType.DMA((2,)),
        ],
        compiler_params=pltpu.CompilerParams(vmem_limit_bytes=24 << 20),
        cost_estimate=pl.CostEstimate(
            flops=4 * taps * group * frame_len * frames * width,
            bytes_accessed=2 * voltages.size,
            transcendentals=0,
        ),
        name="channelize",
    )(me, *(pltpu.with_memory_space_constraint(x, pltpu.HBM) for x in (table, pfb_taps, voltages)))


def with_shares(main, shares, q, taps):
    frames, width = main.shape
    first = frames - (taps - 1)
    late = lax.broadcasted_iota(jnp.int32, (frames, width), 0) >= first
    moved = pltpu.roll(shares, (first - q * taps) % (PARTS * taps), 0)
    return (main.astype(jnp.float32) + jnp.where(late, moved, 0.0)).astype(main.dtype)


def merge_kernel(taps, frames, me_ref, mine, theirs, *outs):
    body, extra = PARTS * frames, PARTS * taps
    size = body + extra

    def emit(even, odd):
        for e, out in enumerate(outs):
            shares = odd[e * size + body : (e + 1) * size, :].astype(jnp.float32)
            for q in range(PARTS):
                at = e * size + q * frames
                out[q * frames : (q + 1) * frames, :] = with_shares(even[at : at + frames, :], shares, q, taps)
            out[body : 2 * body, :] = odd[e * size : e * size + body, :]
            out[2 * body :, :] = even[e * size + body : (e + 1) * size, :]

    is_even = lax.rem(me_ref[0], 2) == 0

    @pl.when(is_even)
    def _():
        emit(mine, theirs)

    @pl.when(jnp.logical_not(is_even))
    def _():
        emit(theirs, mine)


def merge(me, mine, theirs, pairs, taps, frames):
    shape = (PARTS * (2 * frames + taps), mine.shape[1])
    return pl.pallas_call(
        functools.partial(merge_kernel, taps, frames),
        in_specs=[pl.BlockSpec(memory_space=pltpu.SMEM)] + [pl.BlockSpec(memory_space=pltpu.VMEM)] * 2,
        out_specs=[pl.BlockSpec(memory_space=pltpu.VMEM)] * pairs,
        out_shape=[jax.ShapeDtypeStruct(shape, mine.dtype)] * pairs,
        compiler_params=pltpu.CompilerParams(vmem_limit_bytes=8 << 20),
        cost_estimate=pl.CostEstimate(flops=0, bytes_accessed=4 * mine.size, transcendentals=0),
        name="merge",
    )(me, mine, theirs)


def pack_kernel(taps, frames, *refs):
    chips, out = refs[:-1], refs[-1]
    body = PARTS * frames
    for k in range(len(chips) - 1):
        shares = chips[k + 1][2 * body :, :].astype(jnp.float32)
        for q in range(PARTS):
            at = 2 * k * frames
            out[q // 2, q % 2, at : at + frames, :] = chips[k][q * frames : (q + 1) * frames, :]
            odd = chips[k][body + q * frames : body + (q + 1) * frames, :]
            out[q // 2, q % 2, at + frames : at + 2 * frames, :] = with_shares(odd, shares, q, taps)


def pack(chips, taps, frames):
    width = chips[0].shape[1]
    count = len(chips) - 1
    return pl.pallas_call(
        functools.partial(pack_kernel, taps, frames),
        in_specs=[pl.BlockSpec(memory_space=pltpu.VMEM)] * len(chips),
        out_shape=jax.ShapeDtypeStruct((CH_DEV, 2, 2 * count * frames, width), jnp.bfloat16),
        compiler_params=pltpu.CompilerParams(vmem_limit_bytes=8 << 20),
        cost_estimate=pl.CostEstimate(flops=0, bytes_accessed=4 * count * chips[0].size, transcendentals=0),
        name="pack",
    )(*chips)


def fill_left(scale, left, halves):
    for c in range(CH_DEV):
        both = jnp.concatenate([x[c, k] for k in range(2) for x in halves], axis=0).T * scale
        rows, depth = both.shape[0], both.shape[1] // 2
        left[c, :rows, :] = both
        left[c, rows:, :depth] = both[:, depth:]
        left[c, rows:, depth:] = -both[:, :depth]


def correlate_kernel(scales, count, step, index_ref, *refs):
    held, sems = refs[-2:]
    first = len(refs) == 2 * count + 4
    if first:
        blocks, (out, left) = refs[: 2 * count], refs[-4:-2]
        fill_left(scales[0], left, blocks)
    else:
        left, blocks, out = refs[0], refs[1 : 1 + 2 * count], refs[-3]
    rows, width = held.shape[2], held.shape[3]
    parts = width // step
    sent = []
    for k in range(count):
        base = index_ref[k] * width
        for c in range(CH_DEV):
            for n in range(parts):
                cols = slice(n * step, (n + 1) * step)
                right = jnp.concatenate([x[c, p, :, cols] for p in range(2) for x in blocks[2 * k : 2 * k + 2]], axis=0)
                for p in range(2):
                    slot = (k * CH_DEV + c) * 2 + p
                    res = jnp.dot(left[c, p * rows : (p + 1) * rows], right, preferred_element_type=jnp.float32)
                    held[slot // 2, p, :, cols] = res if scales[1] == 1.0 else res * scales[1]
                    copy = pltpu.make_async_copy(
                        held.at[slot // 2, p, :, cols],
                        out.at[c, p, :, pl.ds(pl.multiple_of(base + n * step, step), step)],
                        sems.at[slot * parts + n],
                    )
                    copy.start()
                    sent.append(copy)
    for copy in sent:
        copy.wait()


def correlate(left, blocks, index, so_far, tiles, total):
    chans, _, _, width = blocks[0][0].shape
    count = len(blocks)
    flat = [x for pair in blocks for x in pair]
    full = 2 * sum(x.shape[2] for x in blocks[0])
    step = min(256, width)
    exact = total & (total - 1) == 0
    scales = (1.0 / total, 1.0) if exact else (1.0, 1.0 / total)
    vmem = pl.BlockSpec(memory_space=pltpu.VMEM)
    anywhere = pl.BlockSpec(memory_space=pl.ANY)
    shape = jax.ShapeDtypeStruct((chans, 2, width, tiles * width), jnp.float32)
    first = left is None
    slots = chans * count
    ins = [vmem] * len(flat) if first else [vmem] * (1 + len(flat)) + [anywhere]
    return pl.pallas_call(
        functools.partial(correlate_kernel, scales, count, step),
        in_specs=[pl.BlockSpec(memory_space=pltpu.SMEM)] + ins,
        out_specs=[anywhere, vmem] if first else anywhere,
        out_shape=[shape, jax.ShapeDtypeStruct((chans, 2 * width, full), jnp.bfloat16)] if first else shape,
        scratch_shapes=[
            pltpu.VMEM((slots, 2, width, width), jnp.float32),
            pltpu.SemaphoreType.DMA((2 * slots * (width // step),)),
        ],
        input_output_aliases={} if first else {2 + len(flat): 0},
        compiler_params=pltpu.CompilerParams(vmem_limit_bytes=(2 * slots * width * width * 4) + (8 << 20)),
        cost_estimate=pl.CostEstimate(
            flops=4 * count * chans * width * width * full,
            bytes_accessed=8 * count * chans * width * width,
            transcendentals=0,
        ),
        name="correlate",
    )(*((index, *flat) if first else (index, left, *flat, so_far)))


def turn(block, route):
    return lax.ppermute(block, "chan", route)


def swap(block, bit):
    return lax.ppermute(block, "tile", [(i, i ^ bit) for i in range(lax.axis_size("tile"))])


def shards(voltages, pfb_taps):
    chan_count = lax.axis_size("chan")
    tiles = lax.axis_size("tile")
    taps, frame_len = pfb_taps.shape
    frames = voltages.shape[0] // frame_len
    me = lax.axis_index("chan").astype(jnp.int32).reshape(1)
    pairs = chan_count // 2
    mine, theirs = channelize(voltages, pfb_taps, chan_count)
    theirs = turn(theirs, [(i, i ^ 1) for i in range(chan_count)])
    chips = list(merge(me, mine, theirs, pairs, taps, frames))
    for e in sorted(range(1, pairs), key=lambda e: min(e, pairs - e)):
        chips[e] = turn(chips[e], [(i, (i - 2 * e) % chan_count) for i in range(chan_count)])
    first = -(pairs // 2) + 1

    def stack(distances):
        return pack([chips[e % pairs] for e in [*distances, distances[-1] + 1]], taps, frames)

    halves = [stack(range(first, 1)), stack(range(1, first + pairs))]
    bits = [1 << n for n in range(tiles.bit_length() - 1)]
    blocks = [{0: half} for half in halves]
    for half in blocks:
        for bit in bits:
            half[bit] = swap(half[0], bit)
    for half, order in zip(blocks, (bits, bits[::-1])):
        seen = [0]
        for bit in order:
            for e in seen[1:]:
                half[e | bit] = swap(half[e], bit)
            seen += [e | bit for e in seen]
    total = chan_count * frames
    own = lax.axis_index("tile").astype(jnp.int32)
    out, left = correlate(None, [(blocks[0][0], blocks[1][0])], own.reshape(1), None, tiles, total)
    for group in (bits, [e for e in range(1, tiles) if e not in bits]):
        index = own ^ jnp.array(group, jnp.int32)
        out = correlate(left, [(blocks[0][e], blocks[1][e]) for e in group], index, out, tiles, total)
    return out


def solution(mesh):
    placed = (P("chan", "tile"), P())

    return jax.shard_map(shards, mesh=mesh, in_specs=placed, out_specs=P("chan", None, "tile", None), check_vma=False)
```
